32 devices in a mesh: panel: 16 (over z, x, core), freq: 2 (over y).
Axes of the slice: x: 2, y: 2, z: 4, core: 2. Of those that a mesh axis runs over, the one named last changes fastest.
Arguments:
- sources: bfloat16 [2, 4096, 1024], P(None, ('panel', 'freq')), may hold values from -6 to 6
- panel_pos: float32 [3, 4096], P(None, 'panel'), may hold values from -30 to 30
- normal_angles: float32 [2, 4096], P(None, 'panel'), may hold values from -3.140625 to 3.140625
- observer_angles: float32 [2, 2048], replicated, may hold values from -3.140625 to 3.140625
- absorption: float32 [64, 16], replicated, may hold values from 0.05 to 1
- ray_count: int32 [131072], P('panel'), may hold values from 1 to 8
- ray_layer: int32 [8, 131072], P(None, 'panel'), may hold values from 0 to 15
- ray_length: float32 [8, 131072], P(None, 'panel'), may hold values from 0.1 to 1
- ray_weight: float32 [131072], P('panel'), may hold values from 0.01 to 0.1
- ray_ground: int32 [131072], P('panel'), may hold values from 0 to 4095
Outputs:
- obs_spectrum: float32 [2048, 128], P('panel', 'freq')
- ground_power: float32 [64, 4096], P(None, 'panel')
The draws below stay inside these ranges and needn't reach their ends.
All inputs are finite; a program needn't handle non-finite values.
Results may differ from the reference program's by a relative error of at most 0.0026.
Values may be sent and summed in bfloat16 or wider, within the bound.
A program may use at most 64 MiB of HBM per device.

```python
import math
import jax
import jax.numpy as jnp
from jax import lax

SAMPLES = 1024
FREQS = 64
BIN0 = 32
OBS = 2048
PANELS = 4096
RAYS = 64
RAY_ROWS = 131072
SEGS = 8
LAYERS = 16
GROUND = 4096


def plant(array, rng, least, top_value):
    longest = array.shape.index(max(array.shape))
    spots = []
    for shift in (0, 1):
        where = [jax.random.randint(jax.random.fold_in(rng, axis), (), 0, length) for axis, length in enumerate(array.shape)]
        where[longest] = (where[longest] + shift) % array.shape[longest]
        spots.append(tuple(where))
    return array.at[spots[0]].set(least).at[spots[1]].set(top_value)


def level_of(own_key, extent, split, low, high):
    loudness = 1.0
    for position, parts in split:
        draws = jax.random.uniform(jax.random.fold_in(jax.random.fold_in(own_key, 6), position), (parts,), jnp.float32, low / len(split), high / len(split))
        loudness = loudness * jnp.repeat(jnp.exp(draws), extent[position] // parts).reshape((-1,) + (1,) * (len(extent) - 1 - position))
    return loudness


def gaussian(rng, dims, width, reach, split=(), held_as=jnp.bfloat16):
    factor_of = level_of(rng, dims, split, -0.22, 0.18) if split else 1.0
    values = jax.random.normal(rng, dims, jnp.float32) * width * factor_of
    return jnp.minimum(jnp.maximum(values, -reach), reach).astype(held_as)


def setup_inputs(seed: int = 0) -> dict:
    splits = jax.random.split(jax.random.key(seed), 11)
    sources = gaussian(splits[0], (2, PANELS, SAMPLES), 1.0, 6.0, ((1, 32),))
    panel_pos = jnp.clip(jax.random.uniform(splits[1], (3, PANELS), jnp.float32, -30.0, 30.0) * level_of(splits[1], (3, PANELS), ((1, 16),), -0.4, 0.0), -30.0, 30.0)
    normal_angles = jnp.clip(jax.random.uniform(splits[2], (2, PANELS), jnp.float32, -3.140625, 3.140625), -3.140625, 3.140625)
    observer_angles = jnp.clip(jax.random.uniform(splits[3], (2, OBS), jnp.float32, -3.140625, 3.140625), -3.140625, 3.140625)
    absorption = jnp.clip(jnp.exp(jax.random.uniform(splits[4], (FREQS, LAYERS), jnp.float32, math.log(0.05), math.log(1.0))), 0.05, 1.0)
    ray_count = plant(jax.random.randint(splits[5], (RAY_ROWS,), 1, SEGS + 1), jax.random.fold_in(splits[5], 1), 1, SEGS).astype(jnp.int32)
    ray_layer = plant(jax.random.randint(splits[6], (SEGS, RAY_ROWS), 0, LAYERS), jax.random.fold_in(splits[6], 1), 0, LAYERS - 1).astype(jnp.int32)
    ray_length = jnp.clip(jnp.exp(math.log(1.0) - 2.3025851 * jax.random.uniform(splits[7], (SEGS, RAY_ROWS), jnp.float32) ** level_of(splits[7], (SEGS, RAY_ROWS), ((1, 16),), -0.2, 0.2)), 0.1, 1.0)
    ray_weight = jnp.clip(jnp.exp(math.log(0.1) - 2.3025851 * jax.random.uniform(splits[8], (RAY_ROWS,), jnp.float32) ** level_of(splits[8], (RAY_ROWS,), ((0, 16),), -0.2, 0.2)), 0.01, 0.1)
    ray_ground = plant(jax.random.randint(splits[9], (RAY_ROWS,), 0, GROUND), jax.random.fold_in(splits[9], 1), 0, GROUND - 1).astype(jnp.int32)
    return dict(sources=sources, panel_pos=panel_pos, normal_angles=normal_angles, observer_angles=observer_angles, absorption=absorption, ray_count=ray_count, ray_layer=ray_layer, ray_length=ray_length, ray_weight=ray_weight, ray_ground=ray_ground)


RADIUS = 150.0
GAIN = 3.0

def dft_table(samples, first_bin, nfreqs):
    sample_index = jnp.arange(samples, dtype=jnp.int32)
    bin_index = first_bin + jnp.arange(nfreqs, dtype=jnp.int32)
    phase_turns = sample_index[:, None] * bin_index[None, :] % samples
    phase_angle = 2.0 * math.pi / samples * phase_turns.astype(jnp.float32)
    window = 0.5 - 0.5 * jnp.cos(2.0 * math.pi / samples * sample_index.astype(jnp.float32))
    weighting = (window / math.sqrt(samples))[:, None]
    stacked = jnp.stack([weighting * jnp.cos(phase_angle), -weighting * jnp.sin(phase_angle)], axis=2)
    return stacked.reshape(samples, 2 * nfreqs).astype(jnp.bfloat16)

def sphere_points(angles, radius, downward):
    polar_angle = angles[0]
    azimuth = angles[1]
    height = -jnp.cos(polar_angle) if downward else jnp.cos(polar_angle)
    return radius * jnp.stack([jnp.sin(polar_angle) * jnp.cos(azimuth), jnp.sin(polar_angle) * jnp.sin(azimuth), height])

def radiate(points, panel_pos, normals, wavenumbers, spectra, weighting):
    offset = points[:, :, None] - panel_pos[:, None, :]
    distance = jnp.sqrt(lax.optimization_barrier(jnp.sum(offset * offset, axis=0)))
    inverse = 1.0 / distance
    cosine = lax.optimization_barrier(jnp.sum(offset * normals[:, None, :], axis=0)) * inverse
    amplitude = RADIUS * weighting * inverse
    freq_count = wavenumbers.shape[0]
    per_freq = spectra.reshape(2, spectra.shape[1], freq_count, 2).transpose(2, 0, 1, 3)

    def one_freq(inputs):
        wavenumber, coeffs = inputs
        phase = wavenumber * distance
        cos_part = amplitude * jnp.cos(phase)
        sin_part = -amplitude * jnp.sin(phase)
        dip_real = cosine * (cos_part * inverse - wavenumber * sin_part)
        dip_imag = cosine * (sin_part * inverse + wavenumber * cos_part)
        mono_real = (-wavenumber * coeffs[0, :, 1])[None, :]
        mono_imag = (wavenumber * coeffs[0, :, 0])[None, :]
        load_real = coeffs[1, :, 0][None, :]
        load_imag = coeffs[1, :, 1][None, :]
        real_sum = lax.optimization_barrier(jnp.sum(cos_part * mono_real - sin_part * mono_imag + dip_real * load_real - dip_imag * load_imag, axis=1))
        imag_sum = lax.optimization_barrier(jnp.sum(cos_part * mono_imag + sin_part * mono_real + dip_real * load_imag + dip_imag * load_real, axis=1))
        return jnp.stack([real_sum, imag_sum], axis=1)
    result = lax.map(one_freq, (wavenumbers, per_freq))
    return result.transpose(1, 0, 2).reshape(points.shape[1], 2 * freq_count)

def layer_lengths(ray_count, ray_layer, ray_length):
    seg_rows = ray_layer.shape[0]
    segment = jnp.arange(seg_rows, dtype=jnp.int32)[:, None]
    used = jnp.where(segment < ray_count.reshape(1, -1), ray_length.reshape(seg_rows, -1), 0.0)
    layer_ids = jnp.arange(LAYERS, dtype=jnp.int32)[None, :, None]
    matches = ray_layer.reshape(seg_rows, 1, -1) == layer_ids
    return lax.optimization_barrier(jnp.sum(jnp.where(matches, used[:, None, :], 0.0), axis=0))

def ground_energy(power_rows, absorption, lengths, ray_weight, ray_ground, ground_count):
    optical_depth = jnp.dot(absorption, lengths, precision=lax.Precision.HIGHEST)
    freq_count = power_rows.shape[0]
    obs_count = power_rows.shape[1]
    shaped = optical_depth.reshape(freq_count, obs_count, RAYS)
    energy = power_rows[:, :, None] * ray_weight.reshape(1, obs_count, RAYS) * jnp.exp(-shaped)
    empty = jnp.zeros((freq_count, ground_count), jnp.float32)
    return empty.at[:, ray_ground.reshape(-1)].add(energy.reshape(freq_count, -1))

def reference(sources, panel_pos, normal_angles, observer_angles, absorption, ray_count, ray_layer, ray_length, ray_weight, ray_ground):
    transform_table = dft_table(SAMPLES, BIN0, FREQS)
    spectra = jnp.dot(sources.reshape(-1, SAMPLES), transform_table, preferred_element_type=jnp.float32)
    spectra = spectra.reshape(2, -1, 2 * FREQS)
    wavenumbers = (BIN0 + jnp.arange(FREQS, dtype=jnp.int32)).astype(jnp.float32) * (2.0 * math.pi / SAMPLES)
    points = sphere_points(observer_angles, RADIUS, True)
    normals = sphere_points(normal_angles, 1.0, False)
    weighting = GAIN / math.sqrt(PANELS)
    obs_spectrum = radiate(points, panel_pos, normals, wavenumbers, spectra, weighting)
    power_rows = (obs_spectrum[:, 0::2] * obs_spectrum[:, 0::2] + obs_spectrum[:, 1::2] * obs_spectrum[:, 1::2]).T
    lengths = layer_lengths(ray_count, ray_layer, ray_length)
    ground_power = ground_energy(power_rows, absorption, lengths, ray_weight, ray_ground, GROUND)
    return (obs_spectrum, ground_power)
```

```python
import functools
import math

import jax
import jax.numpy as jnp
import numpy as np
from jax import lax
from jax.experimental import pallas as pl
from jax.experimental.pallas import tpu as pltpu
from jax.sharding import PartitionSpec as P

SAMPLES = 1024
BIN0 = 32
RADIUS = 150.0
GAIN = 3.0
GROUND = 4096
REACH = 52.0
BLOCK = 16
BLOCKS = 3
ORDERS = BLOCK * BLOCKS
UNITS = BLOCK * BLOCKS * (BLOCKS + 1) // 2
TOP = 56
MESH = pl.DeviceIdType.MESH
VMEM = pltpu.MemorySpace.VMEM


def dft_rows(samples, first_bin, groups, per_group):
    index = np.arange(samples)
    bins = first_bin + np.arange(groups * per_group)
    angle = 2.0 * np.pi / samples * (bins[:, None] * index[None, :] % samples)
    window = (0.5 - 0.5 * np.cos(2.0 * np.pi / samples * index)) / math.sqrt(samples)
    rows = np.stack([window * np.cos(angle), -window * np.sin(angle)])
    rows = rows.reshape(2, groups, per_group, samples).transpose(1, 0, 2, 3)
    return rows.reshape(-1, samples).astype(np.float32)


def sincos_turns(turns):
    part = turns - jnp.round(turns)
    square = part * part
    sine = jnp.float32(-(math.pi**11) / math.factorial(11))
    for power in (9, 7, 5, 3, 1):
        sign = 1.0 if power % 4 == 1 else -1.0
        sine = sine * square + sign * math.pi**power / math.factorial(power)
    sine = sine * part
    cosine = jnp.float32(math.pi**12 / math.factorial(12))
    for power in (10, 8, 6, 4, 2, 0):
        sign = 1.0 if power % 4 == 0 else -1.0
        cosine = cosine * square + sign * math.pi**power / math.factorial(power)
    return 1.0 - 2.0 * sine * sine, 2.0 * sine * cosine


def enter(axis, count):
    barrier = pltpu.get_barrier_semaphore()
    me = lax.axis_index(axis)
    for step in range(1, count):
        pl.semaphore_signal(
            barrier, inc=1, device_id={axis: lax.rem(me + step, count)}, device_id_type=MESH
        )
    return barrier


def split_float(value):
    pieces = []
    for _ in range(3):
        pieces.append(value.astype(jnp.bfloat16))
        value = value - pieces[-1].astype(jnp.float32)
    return pieces


def unit_base(block):
    return sum(ORDERS - BLOCK * earlier for earlier in range(block))


def expansion_table(groups, freqs, weighting):
    wave = 2.0 * np.pi / SAMPLES * (BIN0 + np.arange(groups * freqs))
    reach = wave * RADIUS
    below = np.exp(-1j * reach) / reach * 1j
    hankel = [below, (1 / reach + 1j) * below]
    for n in range(1, ORDERS):
        hankel.append((2 * n + 1) / reach * hankel[n] - hankel[n - 1])
    hankel = np.stack(hankel[:ORDERS])
    radial = (RADIUS * weighting) * (-1j * wave)[None] * hankel
    rows = np.zeros((2, groups * freqs, UNITS * 2 * BLOCK))
    start = 2.0
    for m in range(ORDERS):
        if m:
            start *= 4 * m * m / (2 * m * (2 * m + 1))
        norm = start * (np.pi if m else 2 * np.pi)
        block = m // BLOCK
        for n in range(m, ORDERS):
            if n > m:
                norm *= 4 * (n * n - m * m) / (4 * n * n - 1)
            at = (unit_base(block) + n - BLOCK * block) * 2 * BLOCK + m - BLOCK * block
            value = 4 * np.pi / norm * radial[n]
            for side in range(2 if m else 1):
                rows[0, :, at + BLOCK * side] = value.real
                rows[1, :, at + BLOCK * side] = value.imag
    rows = rows.reshape(2, groups, freqs, -1).transpose(1, 0, 2, 3)
    return rows.astype(np.float32)


def times(left, right):
    return (left[0] * right[0] - left[1] * right[1], left[0] * right[1] + left[1] * right[0])


def azimuth_powers(real, imaginary, shape):
    one = (jnp.broadcast_to(real, shape), jnp.broadcast_to(imaginary, shape))
    row = lax.broadcasted_iota(jnp.int32, shape, 0)
    square = times(one, one)
    fourth = times(square, square)
    eighth = times(fourth, fourth)
    first = None
    for bit, power in ((1, one), (2, square), (4, fourth)):
        picked = (jnp.where(row & bit, power[0], 1.0), jnp.where(row & bit, power[1], 0.0))
        first = picked if first is None else times(first, picked)
    tiles = [first]
    for _ in range(ORDERS // 8 - 1):
        tiles.append(times(tiles[-1], eighth))
    seventh = times(times(fourth, square), one)
    before = [(pltpu.roll(first[0], 1, axis=0), pltpu.roll(first[1], 1, axis=0))]
    before += [times(tile, seventh) for tile in tiles[:-1]]
    return tiles, before


def join(tiles, block, part):
    per = BLOCK // 8
    return jnp.concatenate([tile[part] for tile in tiles[block * per : (block + 1) * per]], axis=0)


def radiate_kernel(freqs, panels, lanes, spectra_ref, pos_ref, normal_ref, angle_ref, table_ref,
                   out_ref, directions, basis, moments, radial, sums, mine, theirs, table, weights,
                   parts, landed, table_sem, pair_send, pair_recv, send_sem, recv_sem):
    owners = 2 * parts.shape[0]
    half = owners // 2
    me = lax.axis_index("panel")
    core = lax.rem(me, 2)
    chip = lax.div(me, 2)
    sibling = me + 1 - 2 * core
    group = lax.axis_index("freq")
    step = 2.0 * math.pi / SAMPLES
    fetch = pltpu.make_async_copy(table_ref.at[group], table, table_sem)
    fetch.start()
    barrier = enter("panel", owners)

    def pair_copy(chunk):
        at = pl.ds(pl.multiple_of(chunk * 128, 128), 128)
        return pltpu.make_async_remote_copy(
            src_ref=mine.at[:, at],
            dst_ref=theirs.at[:, at],
            send_sem=pair_send.at[chunk],
            recv_sem=pair_recv.at[chunk],
            device_id={"panel": sibling},
            device_id_type=MESH,
        )

    def transfer(source, target):
        return pltpu.make_async_remote_copy(
            src_ref=parts.at[target],
            dst_ref=landed.at[source],
            send_sem=send_sem.at[target],
            recv_sem=recv_sem.at[source],
            device_id={"panel": 2 * target + core},
            device_id_type=MESH,
        )

    for order in range(half):
        both = angle_ref[:, 2 * order * lanes : 2 * (order + 1) * lanes]
        angle = jnp.where(core == 0, both[:, 0:lanes], both[:, lanes : 2 * lanes])
        cosine, sine = sincos_turns(angle * jnp.float32(0.5 / math.pi))
        to = slice(order * lanes, (order + 1) * lanes)
        directions[0:1, to] = sine[0:1] * cosine[1:2]
        directions[1:2, to] = sine[0:1] * sine[1:2]
        directions[2:3, to] = -cosine[0:1]
    shape = (BLOCK, 128)
    row = lax.broadcasted_iota(jnp.int32, shape, 0)

    def slope(order, block):
        m = (row + BLOCK * block).astype(jnp.float32)
        return (float(order * order) - m * m) * (4.0 / (4.0 * order * order - 1.0))

    wide = 4

    def observe(index, carry):
        lane = [
            pl.ds(pl.multiple_of(index * (128 * wide) + 128 * n, 128), 128) for n in range(wide)
        ]
        powers = [
            azimuth_powers(directions[0:1, at], directions[1:2, at], (8, 128))[0] for at in lane
        ]
        double = [jnp.broadcast_to(2.0 * directions[2:3, at], shape) for at in lane]
        for block in range(BLOCKS):
            first = BLOCK * block
            cosines = [join(tiles, block, 0) for tiles in powers]
            sines = [join(tiles, block, 1) for tiles in powers]
            now = [jnp.where(row == 0, 1.0, 0.0)] * wide
            past = [jnp.zeros(shape, jnp.float32)] * wide
            for order in range(first, ORDERS):
                at_row = (unit_base(block) + order - first) * 2 * BLOCK
                for n in range(wide):
                    basis[at_row : at_row + BLOCK, lane[n]] = (now[n] * cosines[n]).astype(
                        jnp.bfloat16
                    )
                    basis[at_row + BLOCK : at_row + 2 * BLOCK, lane[n]] = (
                        now[n] * sines[n]
                    ).astype(jnp.bfloat16)
                if order + 1 < ORDERS:
                    beta = slope(order, block)
                    for n in range(wide):
                        later = double[n] * now[n] - beta * past[n]
                        if order + 1 - first < BLOCK:
                            later = jnp.where(row == order + 1 - first, 1.0, later)
                        past[n], now[n] = now[n], later
        return carry

    lax.fori_loop(0, half * lanes // (128 * wide), observe, 0)

    def emit(unit, part, at, value):
        high = value.astype(jnp.bfloat16)
        low = (value - high.astype(jnp.float32)).astype(jnp.bfloat16)
        moments[unit, part * BLOCK : (part + 1) * BLOCK, at] = high
        moments[unit, (2 + part) * BLOCK : (3 + part) * BLOCK, at] = low

    def locate(index, carry):
        at = pl.ds(pl.multiple_of(index * 128, 128), 128)
        beside = pl.ds(pl.multiple_of(panels + index * 128, 128), 128)
        place = pos_ref[:, at] * jnp.float32(1.0 / REACH)
        cosine, sine = sincos_turns(normal_ref[:, at] * jnp.float32(0.5 / math.pi))
        normal = [sine[0:1] * cosine[1:2], sine[0:1] * sine[1:2], cosine[0:1]]
        across = sum(place[n : n + 1] * normal[n] for n in range(3))
        square = sum(place[n : n + 1] * place[n : n + 1] for n in range(3))
        tiles, before = azimuth_powers(place[0:1], place[1:2], (8, 128))
        tilt = (jnp.broadcast_to(normal[0], (8, 128)), jnp.broadcast_to(normal[1], (8, 128)))
        turned = [times(value, tilt) for value in before]
        double = jnp.broadcast_to(2.0 * place[2:3], shape)
        lean = jnp.broadcast_to(2.0 * normal[2], shape)
        size = jnp.broadcast_to(square, shape)
        grow = jnp.broadcast_to(2.0 * across, shape)
        for block in range(BLOCKS):
            first = BLOCK * block
            cosines, sines = join(tiles, block, 0), join(tiles, block, 1)
            m = (row + first).astype(jnp.float32)
            cosines_by = join(turned, block, 0) * m
            sines_by = join(turned, block, 1) * m
            now = jnp.where(row == 0, 1.0, 0.0)
            past = rate = rate_past = jnp.zeros(shape, jnp.float32)
            for order in range(first, ORDERS):
                unit = unit_base(block) + order - first
                emit(unit, 0, at, now * cosines)
                emit(unit, 1, at, now * sines)
                emit(unit, 0, beside, rate * cosines + now * cosines_by)
                emit(unit, 1, beside, rate * sines + now * sines_by)
                if order + 1 < ORDERS:
                    beta = slope(order, block)
                    beta_size = beta * size
                    later = double * now - beta_size * past
                    rate_later = (lean * now + double * rate) - (
                        (beta * grow) * past + beta_size * rate_past
                    )
                    if order + 1 - first < BLOCK:
                        later = jnp.where(row == order + 1 - first, 1.0, later)
                    past, now = now, later
                    rate_past, rate = rate, rate_later
        return carry

    lax.fori_loop(0, panels // 128, locate, 0)
    place = pos_ref[...]
    cosine, sine = sincos_turns(normal_ref[...] * jnp.float32(0.5 / math.pi))
    across = (
        sine[0:1] * cosine[1:2] * place[0:1]
        + sine[0:1] * sine[1:2] * place[1:2]
        + cosine[0:1] * place[2:3]
    )
    square = place[0:1] * place[0:1] + place[1:2] * place[1:2] + place[2:3] * place[2:3]
    length = square * lax.rsqrt(jnp.maximum(square, 1e-30))
    bins = lax.broadcasted_iota(jnp.int32, (freqs, panels), 0) + (BIN0 + group * freqs)
    wave = bins.astype(jnp.float32) * jnp.float32(step)
    size = square * jnp.float32(1.0 / REACH**2)
    argument = wave * length
    log_start = (
        12.0 * math.log(10.0)
        - math.lgamma(2 * TOP + 3)
        + (TOP + 1) * math.log(2.0)
        + math.lgamma(TOP + 2)
    )
    kappa = wave * jnp.float32(REACH)
    inverse = 1.0 / kappa
    later = jnp.zeros((freqs, panels), jnp.float32)
    now = jnp.exp(
        TOP * jnp.log(kappa) + jnp.float32(log_start) - argument * argument / (4.0 * TOP + 6.0)
    )
    size = jnp.broadcast_to(size, (freqs, panels))
    for order in range(TOP, 0, -1):
        earlier = (float(2 * order + 1) * inverse) * now - size * later
        later, now = now, earlier
        if order - 1 <= ORDERS:
            radial[order - 1] = now
    near = later * (length * jnp.float32(1.0 / REACH))
    cosine, sine = sincos_turns(argument * jnp.float32(0.5 / math.pi))
    safe = jnp.maximum(argument, 0.05)
    over = 1.0 / safe
    small = argument < 0.05
    zero = jnp.where(small, 1.0 - argument * argument * (1.0 / 6.0), sine * over)
    one = jnp.where(small, argument * (1.0 / 3.0), (sine * over - cosine) * over)
    scale = (now * zero + near * one) / (now * now + near * near)
    heavy = scale * wave

    def both(value):
        return jnp.concatenate([value, value], axis=0)

    monopole = jnp.concatenate(
        [-heavy * spectra_ref[freqs : 2 * freqs], heavy * spectra_ref[0:freqs]], axis=0
    )
    loading = spectra_ref[2 * freqs : 4 * freqs] * both(scale)
    facing = loading * both(-wave * across * jnp.float32(1.0 / REACH))
    loading = loading * jnp.float32(1.0 / REACH)
    sums[0] = monopole
    sums[1] = facing
    sums[2] = loading
    pl.semaphore_wait(barrier, owners - 1)

    def project(blocks, quad, carry):
        values = [[] for _ in range(blocks)]
        for inner in range(4):
            order = quad * 4 + inner
            here, above = both(radial[order]), both(radial[order + 1])
            strength = jnp.concatenate(
                [sums[0] * here + sums[1] * above, sums[2] * here], axis=1
            )
            high = strength.astype(jnp.bfloat16).astype(jnp.float32)
            right = jnp.concatenate([high, strength - high], axis=0).astype(jnp.bfloat16)
            left = jnp.concatenate(
                [moments[unit_base(b) - BLOCK * b + order] for b in range(blocks)], axis=0
            )
            product = lax.dot_general(
                left, right, (((1,), (1,)), ((), ())), preferred_element_type=jnp.float32
            )
            for b in range(blocks):
                begin = 4 * BLOCK * b
                values[b].append(
                    product[begin : begin + 2 * BLOCK]
                    + product[begin + 2 * BLOCK : begin + 4 * BLOCK]
                )
        for b in range(blocks):
            turned = jnp.transpose(jnp.concatenate(values[b], axis=0))
            chunk = (unit_base(b) - BLOCK * b) // 4 + quad
            at = pl.ds(pl.multiple_of(chunk * 128, 128), 128)
            mine[:, at] = turned[0 : 2 * freqs] + turned[2 * freqs : 4 * freqs]
            pair_copy(chunk).start()
        return carry

    per = BLOCK // 4
    for section in range(BLOCKS):
        lax.fori_loop(
            section * per, (section + 1) * per, functools.partial(project, section + 1), 0
        )
    fetch.wait()

    def merge(chunk, carry):
        pair_copy(chunk).wait_recv()
        at = pl.ds(pl.multiple_of(chunk * 128, 128), 128)
        value = mine[:, at] + theirs[:, at]
        real, imaginary = value[0:freqs], value[freqs : 2 * freqs]
        by_real, by_imaginary = table[0, :, at], table[1, :, at]
        value = jnp.concatenate(
            [
                real * by_real - imaginary * by_imaginary,
                real * by_imaginary + imaginary * by_real,
            ],
            axis=0,
        )
        high = value.astype(jnp.bfloat16).astype(jnp.float32)
        weights[:, at] = jnp.concatenate([high, value - high], axis=0).astype(jnp.bfloat16)
        return carry

    lax.fori_loop(0, UNITS // 4, merge, 0)
    each = 2 if half % 2 == 0 else 1

    def field(order, carry):
        pick = lax.rem(lax.div(chip, each) + 1 + order, half // each)
        at = pl.ds(pl.multiple_of(pick * (each * lanes), each * lanes), each * lanes)
        product = jnp.dot(weights[...], basis[:, at], preferred_element_type=jnp.float32)
        product = product[0 : 2 * freqs] + product[2 * freqs : 4 * freqs]
        for side in range(each):
            target = pick * each + side
            parts[target] = product[:, side * lanes : (side + 1) * lanes]

            @pl.when(target != chip)
            def _():
                transfer(chip, target).start()

        return carry

    lax.fori_loop(0, half // each, field, 0)
    total = parts[chip]
    for n in range(1, half):
        source = lax.rem(chip + n, half)
        transfer(source, source).wait_recv()
        total = total + landed[source]
    out_ref[...] = total
    for n in range(1, half):
        target = lax.rem(chip + n, half)
        transfer(target, target).wait_send()

    def drain(chunk, carry):
        pair_copy(chunk).wait_send()
        return carry

    lax.fori_loop(0, UNITS // 4, drain, 0)


def radiate(spectra, positions, normals, angles, owners, groups, weighting):
    panels = spectra.shape[1]
    freqs = spectra.shape[0] // 4
    observers = angles.shape[1]
    lanes = observers // owners
    half = owners // 2
    depth = UNITS * 2 * BLOCK
    table = jnp.asarray(expansion_table(groups, freqs, weighting))
    return pl.pallas_call(
        functools.partial(radiate_kernel, freqs, panels, lanes),
        out_shape=jax.ShapeDtypeStruct((2 * freqs, lanes), jnp.float32),
        in_specs=[pl.BlockSpec(memory_space=VMEM)] * 4 + [pl.BlockSpec(memory_space=pl.ANY)],
        out_specs=pl.BlockSpec(memory_space=VMEM),
        scratch_shapes=[
            pltpu.VMEM((8, half * lanes), jnp.float32),
            pltpu.VMEM((depth, half * lanes), jnp.bfloat16),
            pltpu.VMEM((UNITS, 4 * BLOCK, 2 * panels), jnp.bfloat16),
            pltpu.VMEM((ORDERS + 1, freqs, panels), jnp.float32),
            pltpu.VMEM((3, 2 * freqs, panels), jnp.float32),
            pltpu.VMEM((2 * freqs, depth), jnp.float32),
            pltpu.VMEM((2 * freqs, depth), jnp.float32),
            pltpu.VMEM((2, freqs, depth), jnp.float32),
            pltpu.VMEM((4 * freqs, depth), jnp.bfloat16),
            pltpu.VMEM((half, 2 * freqs, lanes), jnp.float32),
            pltpu.VMEM((half, 2 * freqs, lanes), jnp.float32),
            pltpu.SemaphoreType.DMA,
            pltpu.SemaphoreType.DMA((UNITS // 4,)),
            pltpu.SemaphoreType.DMA((UNITS // 4,)),
            pltpu.SemaphoreType.DMA((half,)),
            pltpu.SemaphoreType.DMA((half,)),
        ],
        compiler_params=pltpu.CompilerParams(
            vmem_limit_bytes=60 * 1024 * 1024,
            collective_id=1,
            has_side_effects=True,
        ),
        name="radiate",
    )(spectra, positions, normals, angles, table)


def ground_kernel(chunk, rays, owners, groups, each, spectrum_ref, absorption_ref, count_ref,
                  layer_ref, length_ref, weight_ref, ground_ref, out_ref, spreading, energies, lows, left,
                  total, own, parts, landed, mine, others, send_sem, recv_sem, send_group,
                  recv_group):
    freqs = absorption_ref.shape[0]
    layers = absorption_ref.shape[1]
    observers = spectrum_ref.shape[1]
    low_size = out_ref.shape[1]
    me = lax.axis_index("panel")
    group = lax.axis_index("freq")
    barrier = enter("panel", owners)
    enter("freq", groups)
    real, imaginary = spectrum_ref[0:freqs, :], spectrum_ref[freqs : 2 * freqs, :]
    power = real * real + imaginary * imaginary
    chunks = count_ref.shape[1] // chunk
    split = split_float(absorption_ref[...])
    absorb = jnp.concatenate([split[i] for i in (0, 0, 1, 0, 1, 2)], axis=1)
    shape = (observers, chunk)
    begin = lax.broadcasted_iota(jnp.int32, shape, 0) * rays
    column = lax.broadcasted_iota(jnp.int32, shape, 1)
    same_owner = (column >= begin) & (column < begin + rays)
    spreading[...] = jnp.where(same_owner, 1.0, 0.0).astype(jnp.bfloat16)

    def transfer(source, target):
        return pltpu.make_async_remote_copy(
            src_ref=parts.at[target],
            dst_ref=landed.at[source],
            send_sem=send_sem.at[target],
            recv_sem=recv_sem.at[source],
            device_id={"panel": target},
            device_id_type=MESH,
        )

    def prepare(index, carry):
        at = pl.ds(pl.multiple_of(index * chunk, chunk), chunk)
        layer_ids = lax.broadcasted_iota(jnp.int32, (layers, chunk), 0)
        count = count_ref[0:1, at]
        lengths = jnp.zeros((layers, chunk), jnp.float32)
        for segment in range(layer_ref.shape[0]):
            used = jnp.where(segment < count, length_ref[segment : segment + 1, at], 0.0)
            same = layer_ref[segment : segment + 1, at] == layer_ids
            lengths = lengths + jnp.where(same, used, 0.0)
        split = split_float(lengths)
        lengths = jnp.concatenate([split[i] for i in (0, 1, 0, 2, 1, 0)], axis=0)
        depth = jnp.dot(absorb, lengths, preferred_element_type=jnp.float32)
        turned = pltpu.roll(power, lax.rem(observers - index * (chunk // rays), observers), axis=1)
        spread = jnp.dot(
            jnp.concatenate(split_float(turned), axis=0),
            spreading[...],
            preferred_element_type=jnp.float32,
        )
        spread = spread[0:freqs] + spread[freqs : 2 * freqs] + spread[2 * freqs : 3 * freqs]
        energy = spread * weight_ref[0:1, at] * jnp.exp(-depth)
        energies[:, at] = energy.astype(jnp.bfloat16)
        within = ground_ref[0:1, at] & (low_size - 1)
        ids = lax.broadcasted_iota(jnp.int32, (low_size, chunk), 0)
        lows[:, at] = jnp.where(ids == within, 1.0, 0.0).astype(jnp.bfloat16)
        return carry

    lax.fori_loop(0, chunks, prepare, 0)
    pl.semaphore_wait(barrier, owners + groups - 2)

    def batch(order, carry):
        base = lax.rem(lax.div(me, each) + 1 + order, owners // each) * each
        total[...] = jnp.zeros_like(total)

        def step(index, carry):
            at = pl.ds(pl.multiple_of(index * chunk, chunk), chunk)
            block = ground_ref[0:1, at] // low_size
            for n in range(each):
                keep = jnp.where(block == base + n, 1.0, 0.0).astype(jnp.bfloat16)
                left[n * freqs : (n + 1) * freqs, :] = energies[:, at] * keep
            total[...] += lax.dot_general(
                left[...],
                lows[:, at],
                (((1,), (1,)), ((), ())),
                preferred_element_type=jnp.float32,
            )
            return carry

        lax.fori_loop(0, chunks, step, 0)
        for n in range(each):
            target = base + n
            value = total[n * freqs : (n + 1) * freqs, :]
            parts[target] = value.astype(jnp.bfloat16)

            @pl.when(target != me)
            def _():
                transfer(me, target).start()

            @pl.when(target == me)
            def _():
                own[...] = value

        return carry

    lax.fori_loop(0, owners // each, batch, 0)
    value = own[...]
    for step in range(1, owners):
        source = lax.rem(me + step, owners)
        transfer(source, source).wait_recv()
        value = value + landed[source].astype(jnp.float32)
    mine[...] = value
    across = []
    for step in range(1, groups):
        peer = lax.rem(group + step, groups)
        across.append(
            pltpu.make_async_remote_copy(
                src_ref=mine,
                dst_ref=others.at[step],
                send_sem=send_group.at[step],
                recv_sem=recv_group.at[step],
                device_id={"freq": peer},
                device_id_type=MESH,
            )
        )
        across[-1].start()
    out_ref[pl.ds(pl.multiple_of(group * freqs, freqs), freqs), :] = value
    for step in range(1, owners):
        target = lax.rem(me + step, owners)
        transfer(target, target).wait_send()
    for step in range(1, groups):
        across[step - 1].wait_recv()
        source = lax.rem(group + groups - step, groups)
        out_ref[pl.ds(pl.multiple_of(source * freqs, freqs), freqs), :] = others[step]
    for copy in across:
        copy.wait_send()


def ground_sums(spectrum, absorption, count, layer, length, weight, ground, owners, groups):
    freqs = absorption.shape[0]
    rows = count.shape[1]
    chunk = 1024
    low_size = GROUND // owners
    rays = rows // spectrum.shape[1]
    each = min(4, owners)
    return pl.pallas_call(
        functools.partial(ground_kernel, chunk, rays, owners, groups, each),
        out_shape=jax.ShapeDtypeStruct((groups * freqs, low_size), jnp.float32),
        in_specs=[pl.BlockSpec(memory_space=VMEM)] * 7,
        out_specs=pl.BlockSpec(memory_space=VMEM),
        scratch_shapes=[
            pltpu.VMEM((spectrum.shape[1], chunk), jnp.bfloat16),
            pltpu.VMEM((freqs, rows), jnp.bfloat16),
            pltpu.VMEM((low_size, rows), jnp.bfloat16),
            pltpu.VMEM((each * freqs, chunk), jnp.bfloat16),
            pltpu.VMEM((each * freqs, low_size), jnp.float32),
            pltpu.VMEM((freqs, low_size), jnp.float32),
            pltpu.VMEM((owners, freqs, low_size), jnp.bfloat16),
            pltpu.VMEM((owners, freqs, low_size), jnp.bfloat16),
            pltpu.VMEM((freqs, low_size), jnp.float32),
            pltpu.VMEM((groups, freqs, low_size), jnp.float32),
            pltpu.SemaphoreType.DMA((owners,)),
            pltpu.SemaphoreType.DMA((owners,)),
            pltpu.SemaphoreType.DMA((groups,)),
            pltpu.SemaphoreType.DMA((groups,)),
        ],
        compiler_params=pltpu.CompilerParams(
            vmem_limit_bytes=48 * 1024 * 1024,
            collective_id=2,
            has_side_effects=True,
        ),
        name="ground",
    )(spectrum, absorption, count, layer, length, weight, ground)


def shards(
    sources,
    panel_pos,
    normal_angles,
    observer_angles,
    absorption,
    ray_count,
    ray_layer,
    ray_length,
    ray_weight,
    ray_ground,
):
    groups = lax.axis_size("freq")
    owners = lax.axis_size("panel")
    freqs = absorption.shape[0] // groups
    freq_start = lax.axis_index("freq") * freqs
    table = jnp.asarray(dft_rows(SAMPLES, BIN0, groups, freqs)).astype(jnp.bfloat16)
    partial_value = lax.dot_general(
        table,
        sources.reshape(-1, SAMPLES),
        (((1,), (1,)), ((), ())),
        preferred_element_type=jnp.float32,
    )
    partial_value = partial_value.reshape(2 * groups * freqs, 2, sources.shape[1])
    spectra = lax.all_to_all(partial_value, "freq", split_axis=0, concat_axis=2, tiled=True)
    spectra = spectra.transpose(1, 0, 2).reshape(4 * freqs, -1)
    weighting = GAIN / math.sqrt(panel_pos.shape[1] * owners)
    spectrum = radiate(
        spectra, panel_pos, normal_angles, observer_angles, owners, groups, weighting
    )
    obs_spectrum = (
        spectrum.reshape(2, freqs, -1).transpose(2, 1, 0).reshape(-1, 2 * freqs)
    )
    own_absorption = lax.dynamic_slice_in_dim(absorption, freq_start, freqs, 0)
    ground_power = ground_sums(
        spectrum,
        own_absorption,
        ray_count.reshape(1, -1),
        ray_layer,
        ray_length,
        ray_weight.reshape(1, -1),
        ray_ground.reshape(1, -1),
        owners,
        groups,
    )
    return (obs_spectrum, ground_power)


def solution(mesh):
    return jax.shard_map(
        shards,
        mesh=mesh,
        in_specs=(
            P(None, ("panel", "freq"), None),
            P(None, "panel"),
            P(None, "panel"),
            P(),
            P(),
            P("panel"),
            P(None, "panel"),
            P(None, "panel"),
            P("panel"),
            P("panel"),
        ),
        out_specs=(P("panel", "freq"), P(None, "panel")),
        check_vma=False,
    )
```

```python
import functools
import math

import jax
import jax.numpy as jnp
import numpy as np
from jax import lax
from jax.experimental import pallas as pl
from jax.experimental.pallas import tpu as pltpu
from jax.sharding import PartitionSpec as P

SAMPLES = 1024
BIN0 = 32
RADIUS = 150.0
GAIN = 3.0
GROUND = 4096
REACH = 52.0
BLOCK = 16
BLOCKS = 3
ORDERS = BLOCK * BLOCKS
UNITS = BLOCK * BLOCKS * (BLOCKS + 1) // 2
TOP = 56
MESH = pl.DeviceIdType.MESH
VMEM = pltpu.MemorySpace.VMEM


def dft_rows(samples, first_bin, groups, per_group):
    index = np.arange(samples)
    bins = first_bin + np.arange(groups * per_group)
    angle = 2.0 * np.pi / samples * (bins[:, None] * index[None, :] % samples)
    window = (0.5 - 0.5 * np.cos(2.0 * np.pi / samples * index)) / math.sqrt(samples)
    rows = np.stack([window * np.cos(angle), -window * np.sin(angle)])
    rows = rows.reshape(2, groups, per_group, samples).transpose(1, 0, 2, 3)
    return rows.reshape(-1, samples).astype(np.float32)


def sincos_turns(turns):
    part = turns - jnp.round(turns)
    square = part * part
    sine = jnp.float32(-(math.pi**11) / math.factorial(11))
    for power in (9, 7, 5, 3, 1):
        sign = 1.0 if power % 4 == 1 else -1.0
        sine = sine * square + sign * math.pi**power / math.factorial(power)
    sine = sine * part
    cosine = jnp.float32(math.pi**12 / math.factorial(12))
    for power in (10, 8, 6, 4, 2, 0):
        sign = 1.0 if power % 4 == 0 else -1.0
        cosine = cosine * square + sign * math.pi**power / math.factorial(power)
    return 1.0 - 2.0 * sine * sine, 2.0 * sine * cosine


def enter(axis, count):
    barrier = pltpu.get_barrier_semaphore()
    me = lax.axis_index(axis)
    for step in range(1, count):
        pl.semaphore_signal(
            barrier, inc=1, device_id={axis: lax.rem(me + step, count)}, device_id_type=MESH
        )
    return barrier


def split_float(value):
    pieces = []
    for _ in range(2):
        pieces.append(value.astype(jnp.bfloat16))
        value = value - pieces[-1].astype(jnp.float32)
    return pieces


def unit_base(block):
    return sum(ORDERS - BLOCK * earlier for earlier in range(block))


def expansion_table(groups, freqs, weighting):
    wave = 2.0 * np.pi / SAMPLES * (BIN0 + np.arange(groups * freqs))
    reach = wave * RADIUS
    below = np.exp(-1j * reach) / reach * 1j
    hankel = [below, (1 / reach + 1j) * below]
    for n in range(1, ORDERS):
        hankel.append((2 * n + 1) / reach * hankel[n] - hankel[n - 1])
    hankel = np.stack(hankel[:ORDERS])
    radial = (RADIUS * weighting) * (-1j * wave)[None] * hankel
    rows = np.zeros((2, groups * freqs, UNITS * 2 * BLOCK))
    start = 2.0
    for m in range(ORDERS):
        if m:
            start *= 4 * m * m / (2 * m * (2 * m + 1))
        norm = start * (np.pi if m else 2 * np.pi)
        block = m // BLOCK
        for n in range(m, ORDERS):
            if n > m:
                norm *= 4 * (n * n - m * m) / (4 * n * n - 1)
            at = (unit_base(block) + n - BLOCK * block) * 2 * BLOCK + m - BLOCK * block
            value = 4 * np.pi / norm * radial[n]
            for side in range(2 if m else 1):
                rows[0, :, at + BLOCK * side] = value.real
                rows[1, :, at + BLOCK * side] = value.imag
    rows = rows.reshape(2, groups, freqs, -1).transpose(1, 0, 2, 3)
    return rows.astype(np.float32)


def times(left, right):
    return (left[0] * right[0] - left[1] * right[1], left[0] * right[1] + left[1] * right[0])


def azimuth_powers(real, imaginary, shape):
    one = (jnp.broadcast_to(real, shape), jnp.broadcast_to(imaginary, shape))
    row = lax.broadcasted_iota(jnp.int32, shape, 0)
    square = times(one, one)
    fourth = times(square, square)
    eighth = times(fourth, fourth)
    first = None
    for bit, power in ((1, one), (2, square), (4, fourth)):
        picked = (jnp.where(row & bit, power[0], 1.0), jnp.where(row & bit, power[1], 0.0))
        first = picked if first is None else times(first, picked)
    tiles = [first]
    for _ in range(ORDERS // 8 - 1):
        tiles.append(times(tiles[-1], eighth))
    seventh = times(times(fourth, square), one)
    before = [(pltpu.roll(first[0], 1, axis=0), pltpu.roll(first[1], 1, axis=0))]
    before += [times(tile, seventh) for tile in tiles[:-1]]
    return tiles, before


def join(tiles, block, part):
    per = BLOCK // 8
    return jnp.concatenate([tile[part] for tile in tiles[block * per : (block + 1) * per]], axis=0)


def kernel(freqs, panels, lanes, sources_hbm, dft_hbm, pos_hbm, normal_hbm, angle_hbm, table_hbm,
           absorption_hbm, count_hbm, layer_hbm, length_hbm, weight_hbm, ground_hbm, spectrum_ref,
           power_ref, sources, dft, pos_ref, normal_ref, angle_ref, table, absorption_ref, count_ref,
           layer_ref, length_ref, weight_ref, ground_ref, outgoing, incoming, directions, basis,
           moments, radial, sums, mine, theirs, weights, parts, landed, upright, damped, spreading,
           energies, lows, left, total, own, pieces, arrived, final, others, fetch_sem, cross_send,
           cross_recv, pair_send, pair_recv, send_sem, recv_sem, piece_send, piece_recv, last_send,
           last_recv):
    owners = 2 * parts.shape[0]
    half = owners // 2
    me = lax.axis_index("panel")
    core = lax.rem(me, 2)
    chip = lax.div(me, 2)
    sibling = me + 1 - 2 * core
    group = lax.axis_index("freq")
    groups = outgoing.shape[0]
    each_part = sources.shape[1]
    step = 2.0 * math.pi / SAMPLES
    pairs = [
        (angle_hbm, angle_ref),
        (sources_hbm, sources),
        (dft_hbm, dft),
        (pos_hbm, pos_ref),
        (normal_hbm, normal_ref),
        (table_hbm.at[group], table),
        (layer_hbm, layer_ref),
        (length_hbm, length_ref),
        (count_hbm, count_ref),
        (weight_hbm, weight_ref),
        (ground_hbm, ground_ref),
        (absorption_hbm, absorption_ref),
    ]
    fetches = [
        pltpu.make_async_copy(pair[0], pair[1], fetch_sem.at[n]) for n, pair in enumerate(pairs)
    ]
    for fetch in fetches:
        fetch.start()
    barrier = enter("panel", owners)
    enter("freq", groups)

    def pair_copy(chunk):
        at = pl.ds(pl.multiple_of(chunk * 128, 128), 128)
        return pltpu.make_async_remote_copy(
            src_ref=mine.at[:, at],
            dst_ref=theirs.at[:, at],
            send_sem=pair_send.at[chunk],
            recv_sem=pair_recv.at[chunk],
            device_id={"panel": sibling},
            device_id_type=MESH,
        )

    def transfer(source, target):
        return pltpu.make_async_remote_copy(
            src_ref=parts.at[target],
            dst_ref=landed.at[source],
            send_sem=send_sem.at[target],
            recv_sem=recv_sem.at[source],
            device_id={"panel": 2 * target + core},
            device_id_type=MESH,
        )

    def cross(source, target):
        return pltpu.make_async_remote_copy(
            src_ref=outgoing.at[target],
            dst_ref=incoming.at[source],
            send_sem=cross_send.at[target],
            recv_sem=cross_recv.at[source],
            device_id={"freq": target},
            device_id_type=MESH,
        )

    fetches[0].wait()
    for order in range(half):
        both = angle_ref[:, 2 * order * lanes : 2 * (order + 1) * lanes]
        angle = jnp.where(core == 0, both[:, 0:lanes], both[:, lanes : 2 * lanes])
        cosine, sine = sincos_turns(angle * jnp.float32(0.5 / math.pi))
        to = slice(order * lanes, (order + 1) * lanes)
        directions[0:1, to] = sine[0:1] * cosine[1:2]
        directions[1:2, to] = sine[0:1] * sine[1:2]
        directions[2:3, to] = -cosine[0:1]
    fetches[1].wait()
    fetches[2].wait()
    lines = jnp.concatenate([sources[0], sources[1]], axis=0)
    bins_of = lax.dot_general(
        dft[...], lines, (((1,), (1,)), ((), ())), preferred_element_type=jnp.float32
    )
    for n in range(groups):
        outgoing[n] = bins_of[n * 2 * freqs : (n + 1) * 2 * freqs]
    pl.semaphore_wait(barrier, owners + groups - 2)
    for n in range(1, groups):
        peer = lax.rem(group + n, groups)
        cross(group, peer).start()
    incoming[group] = outgoing[group]
    row = lax.broadcasted_iota(jnp.int32, (BLOCK, 128), 0)

    def spread_out(value, width):
        return jnp.concatenate([value] * (width // 128), axis=1)

    def slope(order, block, width):
        m = (row + BLOCK * block).astype(jnp.float32)
        value = (float(order * order) - m * m) * (4.0 / (4.0 * order * order - 1.0))
        return spread_out(value, width)

    wide = 512

    def observe(index, carry):
        at = pl.ds(pl.multiple_of(index * wide, wide), wide)
        shape = (BLOCK, wide)
        rows = spread_out(row, wide)
        tiles = azimuth_powers(directions[0:1, at], directions[1:2, at], (8, wide))[0]
        double = jnp.broadcast_to(2.0 * directions[2:3, at], shape)
        for block in range(BLOCKS):
            first = BLOCK * block
            cosines, sines = join(tiles, block, 0), join(tiles, block, 1)
            now = jnp.where(rows == 0, 1.0, 0.0)
            past = jnp.zeros(shape, jnp.float32)
            for order in range(first, ORDERS):
                begin = (unit_base(block) + order - first) * 2 * BLOCK
                basis[begin : begin + BLOCK, at] = (now * cosines).astype(jnp.bfloat16)
                basis[begin + BLOCK : begin + 2 * BLOCK, at] = (now * sines).astype(jnp.bfloat16)
                if order + 1 < ORDERS:
                    later = double * now - slope(order, block, wide) * past
                    if order + 1 - first < BLOCK:
                        later = jnp.where(rows == order + 1 - first, 1.0, later)
                    past, now = now, later
        return carry

    lax.fori_loop(0, half * lanes // wide, observe, 0)

    def emit(unit, part, at, value):
        high = value.astype(jnp.bfloat16)
        low = (value - high.astype(jnp.float32)).astype(jnp.bfloat16)
        moments[unit, part * BLOCK : (part + 1) * BLOCK, at] = high
        moments[unit, (2 + part) * BLOCK : (3 + part) * BLOCK, at] = low

    broad = 256 if panels % 256 == 0 else 128

    def locate(index, carry):
        at = pl.ds(pl.multiple_of(index * broad, broad), broad)
        beside = pl.ds(pl.multiple_of(panels + index * broad, broad), broad)
        shape = (BLOCK, broad)
        rows = spread_out(row, broad)
        place = pos_ref[:, at] * jnp.float32(1.0 / REACH)
        cosine, sine = sincos_turns(normal_ref[:, at] * jnp.float32(0.5 / math.pi))
        normal = [sine[0:1] * cosine[1:2], sine[0:1] * sine[1:2], cosine[0:1]]
        across = sum(place[n : n + 1] * normal[n] for n in range(3))
        square = sum(place[n : n + 1] * place[n : n + 1] for n in range(3))
        tiles, before = azimuth_powers(place[0:1], place[1:2], (8, broad))
        tilt = (
            jnp.broadcast_to(normal[0], (8, broad)),
            jnp.broadcast_to(normal[1], (8, broad)),
        )
        turned = [times(value, tilt) for value in before]
        double = jnp.broadcast_to(2.0 * place[2:3], shape)
        lean = jnp.broadcast_to(2.0 * normal[2], shape)
        size = jnp.broadcast_to(square, shape)
        grow = jnp.broadcast_to(2.0 * across, shape)
        for block in range(BLOCKS):
            first = BLOCK * block
            cosines, sines = join(tiles, block, 0), join(tiles, block, 1)
            m = (rows + first).astype(jnp.float32)
            cosines_by = join(turned, block, 0) * m
            sines_by = join(turned, block, 1) * m
            now = jnp.where(rows == 0, 1.0, 0.0)
            past = rate = rate_past = jnp.zeros(shape, jnp.float32)
            for order in range(first, ORDERS):
                unit = unit_base(block) + order - first
                emit(unit, 0, at, now * cosines)
                emit(unit, 1, at, now * sines)
                emit(unit, 0, beside, rate * cosines + now * cosines_by)
                emit(unit, 1, beside, rate * sines + now * sines_by)
                if order + 1 < ORDERS:
                    beta = slope(order, block, broad)
                    beta_size = beta * size
                    later = double * now - beta_size * past
                    rate_later = (lean * now + double * rate) - (
                        (beta * grow) * past + beta_size * rate_past
                    )
                    if order + 1 - first < BLOCK:
                        later = jnp.where(rows == order + 1 - first, 1.0, later)
                    past, now = now, later
                    rate_past, rate = rate, rate_later
        return carry

    fetches[3].wait()
    fetches[4].wait()
    lax.fori_loop(0, panels // broad, locate, 0)
    place = pos_ref[...]
    cosine, sine = sincos_turns(normal_ref[...] * jnp.float32(0.5 / math.pi))
    across = (
        sine[0:1] * cosine[1:2] * place[0:1]
        + sine[0:1] * sine[1:2] * place[1:2]
        + cosine[0:1] * place[2:3]
    )
    square = place[0:1] * place[0:1] + place[1:2] * place[1:2] + place[2:3] * place[2:3]
    length = square * lax.rsqrt(jnp.maximum(square, 1e-30))
    bins = lax.broadcasted_iota(jnp.int32, (freqs, panels), 0) + (BIN0 + group * freqs)
    wave = bins.astype(jnp.float32) * jnp.float32(step)
    size = square * jnp.float32(1.0 / REACH**2)
    argument = wave * length
    log_start = (
        12.0 * math.log(10.0)
        - math.lgamma(2 * TOP + 3)
        + (TOP + 1) * math.log(2.0)
        + math.lgamma(TOP + 2)
    )
    kappa = wave * jnp.float32(REACH)
    inverse = 1.0 / kappa
    later = jnp.zeros((freqs, panels), jnp.float32)
    now = jnp.exp(
        TOP * jnp.log(kappa) + jnp.float32(log_start) - argument * argument / (4.0 * TOP + 6.0)
    )
    size = jnp.broadcast_to(size, (freqs, panels))
    for order in range(TOP, 0, -1):
        earlier = (float(2 * order + 1) * inverse) * now - size * later
        later, now = now, earlier
        if order - 1 <= ORDERS:
            radial[order - 1] = now
    near = later * (length * jnp.float32(1.0 / REACH))
    cosine, sine = sincos_turns(argument * jnp.float32(0.5 / math.pi))
    safe = jnp.maximum(argument, 0.05)
    over = 1.0 / safe
    small = argument < 0.05
    zero = jnp.where(small, 1.0 - argument * argument * (1.0 / 6.0), sine * over)
    one = jnp.where(small, argument * (1.0 / 3.0), (sine * over - cosine) * over)
    scale = (now * zero + near * one) / (now * now + near * near)
    heavy = scale * wave

    def both(value):
        return jnp.concatenate([value, value], axis=0)

    for n in range(1, groups):
        source = lax.rem(group + n, groups)
        cross(source, source).wait_recv()
    spectra = [
        jnp.concatenate(
            [incoming[n, :, side * each_part : (side + 1) * each_part] for n in range(groups)],
            axis=1,
        )
        for side in range(2)
    ]
    monopole = jnp.concatenate(
        [-heavy * spectra[0][freqs : 2 * freqs], heavy * spectra[0][0:freqs]], axis=0
    )
    loading = spectra[1] * both(scale)
    facing = loading * both(-wave * across * jnp.float32(1.0 / REACH))
    loading = loading * jnp.float32(1.0 / REACH)
    sums[0] = monopole
    sums[1] = facing
    sums[2] = loading

    def project(blocks, quad, carry):
        values = [[] for _ in range(blocks)]
        for inner in range(4):
            order = quad * 4 + inner
            here, above = both(radial[order]), both(radial[order + 1])
            strength = jnp.concatenate(
                [sums[0] * here + sums[1] * above, sums[2] * here], axis=1
            )
            high = strength.astype(jnp.bfloat16).astype(jnp.float32)
            right = jnp.concatenate([high, strength - high], axis=0).astype(jnp.bfloat16)
            left = jnp.concatenate(
                [moments[unit_base(b) - BLOCK * b + order] for b in range(blocks)], axis=0
            )
            product = lax.dot_general(
                left, right, (((1,), (1,)), ((), ())), preferred_element_type=jnp.float32
            )
            for b in range(blocks):
                begin = 4 * BLOCK * b
                values[b].append(
                    product[begin : begin + 2 * BLOCK]
                    + product[begin + 2 * BLOCK : begin + 4 * BLOCK]
                )
        for b in range(blocks):
            turned = jnp.transpose(jnp.concatenate(values[b], axis=0))
            chunk = (unit_base(b) - BLOCK * b) // 4 + quad
            at = pl.ds(pl.multiple_of(chunk * 128, 128), 128)
            mine[:, at] = turned[0 : 2 * freqs] + turned[2 * freqs : 4 * freqs]
            pair_copy(chunk).start()
        return carry

    per = BLOCK // 4
    for section in range(BLOCKS):
        lax.fori_loop(
            section * per, (section + 1) * per, functools.partial(project, section + 1), 0
        )
    fetches[5].wait()

    def merge(chunk, carry):
        pair_copy(chunk).wait_recv()
        at = pl.ds(pl.multiple_of(chunk * 128, 128), 128)
        value = mine[:, at] + theirs[:, at]
        real, imaginary = value[0:freqs], value[freqs : 2 * freqs]
        by_real, by_imaginary = table[0, :, at], table[1, :, at]
        value = jnp.concatenate(
            [
                real * by_real - imaginary * by_imaginary,
                real * by_imaginary + imaginary * by_real,
            ],
            axis=0,
        )
        high = value.astype(jnp.bfloat16).astype(jnp.float32)
        weights[:, at] = jnp.concatenate([high, value - high], axis=0).astype(jnp.bfloat16)
        return carry

    lax.fori_loop(0, UNITS // 4, merge, 0)
    each = 2 if half % 2 == 0 else 1

    def field(order, carry):
        pick = lax.rem(lax.div(chip, each) + 1 + order, half // each)
        at = pl.ds(pl.multiple_of(pick * (each * lanes), each * lanes), each * lanes)
        product = jnp.dot(weights[...], basis[:, at], preferred_element_type=jnp.float32)
        product = product[0 : 2 * freqs] + product[2 * freqs : 4 * freqs]
        for side in range(each):
            target = pick * each + side
            parts[target] = product[:, side * lanes : (side + 1) * lanes]

            @pl.when(target != chip)
            def _():
                transfer(chip, target).start()

        return carry

    lax.fori_loop(0, half // each, field, 0)
    for fetch in fetches[6:]:
        fetch.wait()
    observers = lanes
    rays_all = count_ref.shape[1]
    rays = rays_all // observers
    chunk = left.shape[1]
    chunks = rays_all // chunk
    each_batch = left.shape[0] // freqs
    layers = absorption_ref.shape[0]
    low_size = power_ref.shape[1]
    upright[...] = jnp.transpose(absorption_ref[...])
    split = split_float(upright[pl.ds(pl.multiple_of(group * freqs, freqs), freqs), :])
    absorb = jnp.concatenate([split[i] for i in (0, 0, 1)], axis=1)
    wide_shape = (observers, chunk)
    begin = lax.broadcasted_iota(jnp.int32, wide_shape, 0) * rays
    column = lax.broadcasted_iota(jnp.int32, wide_shape, 1)
    same_owner = (column >= begin) & (column < begin + rays)
    spreading[...] = jnp.where(same_owner, 1.0, 0.0).astype(jnp.bfloat16)

    def piece_copy(source, target):
        return pltpu.make_async_remote_copy(
            src_ref=pieces.at[target],
            dst_ref=arrived.at[source],
            send_sem=piece_send.at[target],
            recv_sem=piece_recv.at[source],
            device_id={"panel": target},
            device_id_type=MESH,
        )

    def prepare(index, carry):
        at = pl.ds(pl.multiple_of(index * chunk, chunk), chunk)
        layer_ids = lax.broadcasted_iota(jnp.int32, (layers, chunk), 0)
        count = count_ref[0:1, at]
        lengths = jnp.zeros((layers, chunk), jnp.float32)
        for segment in range(layer_ref.shape[0]):
            used = jnp.where(segment < count, length_ref[segment : segment + 1, at], 0.0)
            same = layer_ref[segment : segment + 1, at] == layer_ids
            lengths = lengths + jnp.where(same, used, 0.0)
        split = split_float(lengths)
        lengths = jnp.concatenate([split[i] for i in (0, 1, 0)], axis=0)
        depth = jnp.dot(absorb, lengths, preferred_element_type=jnp.float32)
        damped[:, at] = weight_ref[0:1, at] * jnp.exp(-depth)
        within = ground_ref[0:1, at] & (low_size - 1)
        ids = lax.broadcasted_iota(jnp.int32, (low_size, chunk), 0)
        lows[:, at] = jnp.where(ids == within, 1.0, 0.0).astype(jnp.bfloat16)
        return carry

    lax.fori_loop(0, chunks, prepare, 0)
    value = parts[chip]
    for n in range(1, half):
        source = lax.rem(chip + n, half)
        transfer(source, source).wait_recv()
        value = value + landed[source]
    real, imaginary = value[0:freqs], value[freqs : 2 * freqs]
    spectrum_ref[pl.ds(0, freqs, 2), :] = real
    spectrum_ref[pl.ds(1, freqs, 2), :] = imaginary
    power = real * real + imaginary * imaginary

    def spread(index, carry):
        at = pl.ds(pl.multiple_of(index * chunk, chunk), chunk)
        turned = pltpu.roll(power, lax.rem(observers - index * (chunk // rays), observers), axis=1)
        value = jnp.dot(
            jnp.concatenate(split_float(turned), axis=0),
            spreading[...],
            preferred_element_type=jnp.float32,
        )
        value = value[0:freqs] + value[freqs : 2 * freqs]
        energies[:, at] = (value * damped[:, at]).astype(jnp.bfloat16)
        return carry

    lax.fori_loop(0, chunks, spread, 0)

    def batch(order, carry):
        base = lax.rem(lax.div(me, each_batch) + 1 + order, owners // each_batch) * each_batch
        total[...] = jnp.zeros_like(total)

        def accumulate(index, carry):
            at = pl.ds(pl.multiple_of(index * chunk, chunk), chunk)
            block = ground_ref[0:1, at] // low_size
            for n in range(each_batch):
                keep = jnp.where(block == base + n, 1.0, 0.0).astype(jnp.bfloat16)
                left[n * freqs : (n + 1) * freqs, :] = energies[:, at] * keep
            total[...] += lax.dot_general(
                left[...],
                lows[:, at],
                (((1,), (1,)), ((), ())),
                preferred_element_type=jnp.float32,
            )
            return carry

        lax.fori_loop(0, chunks, accumulate, 0)
        for n in range(each_batch):
            target = base + n
            value = total[n * freqs : (n + 1) * freqs, :]
            pieces[target] = value.astype(jnp.bfloat16)

            @pl.when(target != me)
            def _():
                piece_copy(me, target).start()

            @pl.when(target == me)
            def _():
                own[...] = value

        return carry

    lax.fori_loop(0, owners // each_batch, batch, 0)
    value = own[...]
    for n in range(1, owners):
        source = lax.rem(me + n, owners)
        piece_copy(source, source).wait_recv()
        value = value + arrived[source].astype(jnp.float32)
    final[...] = value
    across_copies = []
    for n in range(1, groups):
        across_copies.append(
            pltpu.make_async_remote_copy(
                src_ref=final,
                dst_ref=others.at[n],
                send_sem=last_send.at[n],
                recv_sem=last_recv.at[n],
                device_id={"freq": lax.rem(group + n, groups)},
                device_id_type=MESH,
            )
        )
        across_copies[-1].start()
    power_ref[pl.ds(pl.multiple_of(group * freqs, freqs), freqs), :] = value
    for n in range(1, groups):
        peer = lax.rem(group + n, groups)
        cross(peer, peer).wait_send()
    for n in range(1, half):
        target = lax.rem(chip + n, half)
        transfer(target, target).wait_send()
    for n in range(1, owners):
        target = lax.rem(me + n, owners)
        piece_copy(target, target).wait_send()

    def drain(chunk, carry):
        pair_copy(chunk).wait_send()
        return carry

    lax.fori_loop(0, UNITS // 4, drain, 0)
    for n in range(1, groups):
        across_copies[n - 1].wait_recv()
        source = lax.rem(group + groups - n, groups)
        power_ref[pl.ds(pl.multiple_of(source * freqs, freqs), freqs), :] = others[n]
    for copy in across_copies:
        copy.wait_send()


def shards(
    sources,
    panel_pos,
    normal_angles,
    observer_angles,
    absorption,
    ray_count,
    ray_layer,
    ray_length,
    ray_weight,
    ray_ground,
):
    groups = lax.axis_size("freq")
    owners = lax.axis_size("panel")
    freqs = absorption.shape[0] // groups
    panels = panel_pos.shape[1]
    observers = observer_angles.shape[1]
    lanes = observers // owners
    half = owners // 2
    depth = UNITS * 2 * BLOCK
    rows = ray_count.shape[0]
    chunk = 1024
    low_size = GROUND // owners
    each = min(8, owners)
    weighting = GAIN / math.sqrt(panels * owners)
    dft = jnp.asarray(dft_rows(SAMPLES, BIN0, groups, freqs).astype(jnp.bfloat16))
    table = jnp.asarray(expansion_table(groups, freqs, weighting))
    operands = (
        sources,
        dft,
        panel_pos,
        normal_angles,
        observer_angles,
        table,
        absorption.T,
        ray_count.reshape(1, -1),
        ray_layer,
        ray_length,
        ray_weight.reshape(1, -1),
        ray_ground.reshape(1, -1),
    )
    held = [pltpu.VMEM(value.shape, value.dtype) for value in operands]
    held[5] = pltpu.VMEM(table.shape[1:], table.dtype)
    width = 2 * sources.shape[1]
    f32, bf16 = jnp.float32, jnp.bfloat16
    spectrum, power = pl.pallas_call(
        functools.partial(kernel, freqs, panels, lanes),
        out_shape=(
            jax.ShapeDtypeStruct((2 * freqs, lanes), f32),
            jax.ShapeDtypeStruct((groups * freqs, low_size), f32),
        ),
        in_specs=[pl.BlockSpec(memory_space=pltpu.MemorySpace.HBM)] * len(operands),
        out_specs=(pl.BlockSpec(memory_space=VMEM),) * 2,
        scratch_shapes=held
        + [
            pltpu.VMEM((groups, 2 * freqs, width), f32),
            pltpu.VMEM((groups, 2 * freqs, width), f32),
            pltpu.VMEM((8, half * lanes), f32),
            pltpu.VMEM((depth, half * lanes), bf16),
            pltpu.VMEM((UNITS, 4 * BLOCK, 2 * panels), bf16),
            pltpu.VMEM((ORDERS + 1, freqs, panels), f32),
            pltpu.VMEM((3, 2 * freqs, panels), f32),
            pltpu.VMEM((2 * freqs, depth), f32),
            pltpu.VMEM((2 * freqs, depth), f32),
            pltpu.VMEM((4 * freqs, depth), bf16),
            pltpu.VMEM((half, 2 * freqs, lanes), f32),
            pltpu.VMEM((half, 2 * freqs, lanes), f32),
            pltpu.VMEM(absorption.shape, f32),
            pltpu.VMEM((freqs, rows), f32),
            pltpu.VMEM((lanes, chunk), bf16),
            pltpu.VMEM((freqs, rows), bf16),
            pltpu.VMEM((low_size, rows), bf16),
            pltpu.VMEM((each * freqs, chunk), bf16),
            pltpu.VMEM((each * freqs, low_size), f32),
            pltpu.VMEM((freqs, low_size), f32),
            pltpu.VMEM((owners, freqs, low_size), bf16),
            pltpu.VMEM((owners, freqs, low_size), bf16),
            pltpu.VMEM((freqs, low_size), f32),
            pltpu.VMEM((groups, freqs, low_size), f32),
            pltpu.SemaphoreType.DMA((len(operands),)),
            pltpu.SemaphoreType.DMA((groups,)),
            pltpu.SemaphoreType.DMA((groups,)),
            pltpu.SemaphoreType.DMA((UNITS // 4,)),
            pltpu.SemaphoreType.DMA((UNITS // 4,)),
            pltpu.SemaphoreType.DMA((half,)),
            pltpu.SemaphoreType.DMA((half,)),
            pltpu.SemaphoreType.DMA((owners,)),
            pltpu.SemaphoreType.DMA((owners,)),
            pltpu.SemaphoreType.DMA((groups,)),
            pltpu.SemaphoreType.DMA((groups,)),
        ],
        compiler_params=pltpu.CompilerParams(
            vmem_limit_bytes=65275 * 1024,
            collective_id=1,
            has_side_effects=True,
        ),
        name="spectra",
    )(*operands)
    return spectrum.T, power


def solution(mesh):
    return jax.shard_map(
        shards,
        mesh=mesh,
        in_specs=(
            P(None, ("panel", "freq"), None),
            P(None, "panel"),
            P(None, "panel"),
            P(),
            P(),
            P("panel"),
            P(None, "panel"),
            P(None, "panel"),
            P("panel"),
            P("panel"),
        ),
        out_specs=(P("panel", "freq"), P(None, "panel")),
        check_vma=False,
    )
```
